32 devices in a mesh: row: 16 (over z, x, core), col: 2 (over y).
Axes of the slice: x: 2, y: 2, z: 4, core: 2. Of those that a mesh axis runs over, the one named last changes fastest.
Arguments:
- features: bfloat16 [8192, 256], P(('row', 'col')), may hold values from -6 to 6
- degrees: int32 [8192], P(('row', 'col')), may hold values from 1 to 64
- blocks: bfloat16 [256, 16, 128, 128], P('row', 'col'), may hold values from 0 to 2
- block_ids: int32 [256, 16], P('row', 'col'), may hold values from 0 to 7, as said below
- counts: int32 [256, 2], P('row', 'col'), may hold values from 1 to 8, as said below
- weight: bfloat16 [256, 256], replicated, may hold values from -0.375 to 0.375
- out_bias: float32 [256], replicated, may hold values from -3 to 3
Outputs:
- mixed: bfloat16 [8192, 256], P(('row', 'col'))
The draws below stay inside these ranges and needn't reach their ends.
Inputs may be any that keep to these rules, and one draw needn't show every extreme that they name: `block_ids`: within each list of 8 slots (live or not) the codes are distinct. `counts`: every tile has one segment whose list is full.
All inputs are finite; a program needn't handle non-finite values.
Results may differ from the reference program's by a relative error of at most 0.018.
Values may be sent and summed in bfloat16 or wider, within the bound.
No kernel may reach another device: no remote copies, remote signals or barrier semaphores. Data moves between devices by JAX's collectives and lax.ppermute only.
A program may use at most 128 MiB of HBM per device.

```python
import jax
import jax.numpy as jnp
from jax import lax

FEAT = 256
BS = 128
ROWS_DEV = 256
GRIDROWS = 16
GRIDCOLS = 2
SUBTOTAL = 256
MAXS = 8
NODES = 8192


def draw_blocks(key, part):
    shape = (SUBTOTAL, GRIDCOLS * MAXS, BS, BS)
    logs = jax.random.uniform(jax.random.fold_in(key, 31), shape, jnp.float32, jnp.log(0.1), jnp.log(2.0))
    present = jax.random.uniform(jax.random.fold_in(key, 32), shape, jnp.float32) < 0.25
    return jnp.where(present, jnp.exp(logs), 0.0).astype(jnp.bfloat16)


def draw_block_ids(key, part):
    per_segment = ROWS_DEV // BS * (ROWS_DEV * GRIDCOLS // BS)
    keys = jax.random.split(jax.random.fold_in(key, 11), SUBTOTAL * GRIDCOLS)

    def single(single_key):
        return jax.random.permutation(single_key, per_segment)[:MAXS]
    chosen = jax.vmap(single)(keys)
    return chosen.reshape(SUBTOTAL, GRIDCOLS * MAXS).astype(jnp.int32)


def draw_counts(key, part):
    uniform_part = jax.random.randint(jax.random.fold_in(key, 21), (GRIDROWS, GRIDROWS, GRIDCOLS), 0, MAXS)
    factor = jax.random.randint(jax.random.fold_in(key, 22), (GRIDROWS, 1, GRIDCOLS), 1, 5)
    filled = 1 + uniform_part * factor // 4
    full_at = jax.random.randint(jax.random.fold_in(key, 23), (GRIDROWS, 1, GRIDCOLS), 0, GRIDROWS)
    filled = jnp.where(jnp.arange(GRIDROWS)[None, :, None] == full_at, MAXS, filled)
    return filled.reshape(SUBTOTAL, GRIDCOLS).astype(jnp.int32)


def set_ends(values, own_key, low, largest):
    longest = values.shape.index(max(values.shape))
    spots = []
    for shift in (0, 1):
        where = [jax.random.randint(jax.random.fold_in(own_key, axis), (), 0, length) for axis, length in enumerate(values.shape)]
        where[longest] = (where[longest] + shift) % values.shape[longest]
        spots.append(tuple(where))
    return values.at[spots[0]].set(low).at[spots[1]].set(largest)


def shard_levels(key, dims, shards, least, top_value):
    level, own = 1.0, jax.random.fold_in(key, 6)
    for position, blocks in shards:
        heights = jnp.exp(jax.random.uniform(jax.random.fold_in(own, position), (blocks,), jnp.float32, least / len(shards), top_value / len(shards)))
        level = level * jnp.repeat(heights, dims[position] // blocks).reshape([-1 if axis == position else 1 for axis in range(len(dims))])
    return level


def scatter_about(key, shape, scale, most, cuts=(), held_as=jnp.bfloat16):
    factor_of = shard_levels(key, shape, cuts, -0.22, 0.18) if cuts else 1.0
    values = jax.random.normal(key, shape, jnp.float32) * scale * factor_of
    return jnp.minimum(jnp.maximum(values, -most), most).astype(held_as)


def setup_inputs(seed: int = 0) -> dict:
    splits = jax.random.split(jax.random.key(seed), 8)
    features = scatter_about(splits[0], (NODES, FEAT), 1.0, 6.0, ((0, 32),))
    degrees = set_ends(jax.random.randint(splits[1], (NODES,), 1, 65), jax.random.fold_in(splits[1], 1), 1, 64).astype(jnp.int32)
    blocks = draw_blocks(jax.random.fold_in(splits[7], 71), 0)
    block_ids = draw_block_ids(jax.random.fold_in(splits[7], 71), 0)
    counts = draw_counts(jax.random.fold_in(splits[7], 71), 0)
    weight = scatter_about(splits[5], (FEAT, FEAT), FEAT ** -0.5, 0.375)
    out_bias = scatter_about(splits[6], (FEAT,), 0.5, 3.0, (), jnp.float32)
    return dict(features=features, degrees=degrees, blocks=blocks, block_ids=block_ids, counts=counts, weight=weight, out_bias=out_bias)


def slot_term(block_vals, slot_codes, live_count, gathered):
    col_blocks = gathered.shape[0] // BS
    row_blocks = ROWS_DEV // BS
    col_place = slot_codes % col_blocks
    row_place = slot_codes // col_blocks
    pieces = jnp.take(gathered.reshape(col_blocks, BS, FEAT), col_place, axis=0)
    products = jnp.einsum('kij,kjf->kif', block_vals.astype(jnp.float32), pieces.astype(jnp.float32), precision=lax.Precision.HIGHEST)
    occupied = jnp.arange(slot_codes.shape[0]).astype(jnp.int32) < live_count
    select = ((row_place[:, None] == jnp.arange(row_blocks).astype(jnp.int32)[None, :]) & occupied[:, None]).astype(jnp.float32)
    summed = jnp.einsum('kr,kif->rif', select, products, precision=lax.Precision.HIGHEST)
    return summed.reshape(ROWS_DEV, FEAT)

def reference(features, degrees, blocks, block_ids, counts, weight, out_bias):
    scaling = lax.rsqrt(degrees.astype(jnp.float32))[:, None]
    scaled = (features.astype(jnp.float32) * scaling).astype(jnp.bfloat16)
    group_rows = ROWS_DEV * GRIDCOLS
    shaped_blocks = blocks.reshape(SUBTOTAL, GRIDCOLS, MAXS, BS, BS)
    shaped_codes = block_ids.reshape(SUBTOTAL, GRIDCOLS, MAXS)

    def visit(pair_index, totals):
        pair_index = jnp.asarray(pair_index).astype(jnp.int32)
        entry_row = pair_index // GRIDCOLS
        column = pair_index % GRIDCOLS
        grid_row = entry_row // GRIDROWS
        subrange = entry_row % GRIDROWS
        gathered = lax.dynamic_slice_in_dim(scaled, (grid_row * group_rows).astype(jnp.int32), group_rows, 0)
        contrib = slot_term(shaped_blocks[entry_row, column], shaped_codes[entry_row, column], counts[entry_row, column], gathered)
        contrib = lax.optimization_barrier(contrib.astype(jnp.bfloat16)).astype(jnp.float32)
        offset = ((subrange * GRIDCOLS + column) * ROWS_DEV).astype(jnp.int32)
        current = lax.dynamic_slice_in_dim(totals, offset, ROWS_DEV, 0)
        return lax.dynamic_update_slice_in_dim(totals, current + contrib, offset, 0)
    summed = lax.fori_loop(0, SUBTOTAL * GRIDCOLS, visit, jnp.zeros((NODES, FEAT), jnp.float32))
    combined = (scaling * (summed + scaled.astype(jnp.float32))).astype(jnp.bfloat16)
    mixed = jnp.dot(combined, weight, preferred_element_type=jnp.float32) + out_bias.astype(jnp.float32)
    return jnp.maximum(mixed, 0.0).astype(jnp.bfloat16)
```

```python
import functools

import jax
import jax.numpy as jnp
from jax import lax
from jax.experimental import pallas as pl
from jax.experimental.pallas import tpu as pltpu
from jax.sharding import PartitionSpec as P


def swap_with(value, axis, flip):
    size = lax.axis_size(axis)
    return lax.ppermute(value, axis, [(i, i ^ flip) for i in range(size)])


def from_ahead(value, axis, distance):
    size = lax.axis_size(axis)
    return lax.ppermute(value, axis, [((i + distance) % size, i) for i in range(size)])


def arrange_kernel(orders, geometry, place_ref, ids_ref, counts_ref, blocks_ref, *rest):
    side, row_blocks, col_blocks = geometry
    outs, (stage, sems) = rest[: len(orders)], rest[len(orders) :]
    slots = stage.shape[1]
    me, shift = place_ref[0], place_ref[1]
    flat = [delta for order in orders for delta in order]

    def fetch(spot, delta):
        return pltpu.make_async_copy(blocks_ref.at[me ^ delta], stage.at[spot], sems.at[spot])

    for spot, delta in enumerate(flat):
        fetch(spot, delta).start()
    if slots != row_blocks * col_blocks:
        for out in outs:
            out[...] = jnp.zeros(out.shape, out.dtype)
    spot = 0
    for out, order in zip(outs, orders):
        for position, delta in enumerate(order):
            segment = me ^ delta
            live = counts_ref[segment, 0]
            fetch(spot, delta).wait()
            for slot in range(slots):
                code = ids_ref[segment, slot]
                down = code // col_blocks
                across = lax.rem(lax.rem(code, col_blocks) + shift, col_blocks)
                values = stage[spot, slot]
                values = jnp.where(slot < live, values, jnp.zeros_like(values))
                rows = pl.ds(pl.multiple_of((position * row_blocks + down) * side, side), side)
                lanes = pl.ds(pl.multiple_of(across * side, side), side)
                out[rows, lanes] = values
            spot += 1


def arrange(blocks, block_ids, counts, orders, seg_rows, group_rows, place):
    segments, slots, side, _ = blocks.shape
    geometry = (side, seg_rows // side, group_rows // side)
    total = sum(len(order) for order in orders)
    smem = pl.BlockSpec(memory_space=pltpu.SMEM)
    nbytes = total * seg_rows * group_rows * blocks.dtype.itemsize
    held = nbytes + total * slots * side * side * blocks.dtype.itemsize
    return pl.pallas_call(
        functools.partial(arrange_kernel, orders, geometry),
        out_shape=[jax.ShapeDtypeStruct((len(order) * seg_rows, group_rows), blocks.dtype) for order in orders],
        in_specs=[smem, smem, smem, pl.BlockSpec(memory_space=pl.ANY)],
        out_specs=[pl.BlockSpec(memory_space=pltpu.VMEM) for _ in orders],
        scratch_shapes=[
            pltpu.VMEM((total, slots, side, side), blocks.dtype),
            pltpu.SemaphoreType.DMA((total,)),
        ],
        compiler_params=pltpu.CompilerParams(vmem_limit_bytes=held + (4 << 20)),
        cost_estimate=pl.CostEstimate(flops=0, bytes_accessed=2 * nbytes, transcendentals=0),
    )(place, block_ids, counts, blocks)


def local(features, degrees, blocks, block_ids, counts, weight, out_bias):
    seg_rows, width = features.shape
    rows, cols = lax.axis_size("row"), lax.axis_size("col")
    me, column = lax.axis_index("row"), lax.axis_index("col")
    high = rows // 8
    side = blocks.shape[-1]
    col_blocks = cols * seg_rows // side

    scaling = lax.rsqrt(degrees.astype(jnp.float32))[:, None]
    scaled = (features.astype(jnp.float32) * scaling).astype(jnp.bfloat16)
    parts = [scaled] + [from_ahead(scaled, "col", step) for step in range(1, cols)]

    far = tuple((h * 4 + q) * 2 for h in range(1, high) for q in range(4))
    near = tuple(q * 2 for q in range(4))
    orders = (tuple(d | 1 for d in far), tuple(d | 1 for d in near), far, near)
    shift = (cols - column) * (seg_rows // side) % col_blocks
    place = jnp.stack([me, shift]).astype(jnp.int32)
    dense = arrange(blocks, block_ids, counts, orders, seg_rows, cols * seg_rows, place)

    gathered = jnp.concatenate(parts, axis=0)

    def term(matrix):
        product = jnp.dot(matrix, gathered, preferred_element_type=jnp.float32).astype(jnp.bfloat16)
        return product.reshape(-1, seg_rows, width)

    def add(*values):
        return functools.reduce(jnp.add, [v.astype(jnp.float32) for v in values])

    sent_far = swap_with(term(dense[0]), "row", 1)
    sent_near = swap_with(term(dense[1]), "row", 1)
    chip_far = add(term(dense[2]), sent_far).astype(jnp.bfloat16).reshape(high - 1, 4, seg_rows, width)
    chip_near = add(term(dense[3]), sent_near)
    got_far = [swap_with(chip_far[:, q], "row", 2 * q) for q in range(1, 4)]
    got_near = [swap_with(chip_near[q].astype(jnp.bfloat16), "row", 2 * q) for q in range(1, 4)]
    quad_far = add(chip_far[:, 0], *got_far).astype(jnp.bfloat16)
    own = add(chip_near[0], *got_near)
    for h in range(1, high):
        own = own + swap_with(quad_far[h - 1], "row", 8 * h).astype(jnp.float32)

    combined = (scaling * (own + scaled.astype(jnp.float32))).astype(jnp.bfloat16)
    mixed = jnp.dot(combined, weight, preferred_element_type=jnp.float32) + out_bias
    return jnp.maximum(mixed, 0.0).astype(jnp.bfloat16)


def solution(mesh):
    placed = (
        P(("row", "col"), None),
        P(("row", "col")),
        P("row", "col", None, None),
        P("row", "col"),
        P("row", "col"),
        P(),
        P(),
    )
    return jax.shard_map(
        local, mesh=mesh, in_specs=placed, out_specs=P(("row", "col"), None), check_vma=False
    )
```

```python
import functools

import jax
import jax.numpy as jnp
from jax import lax
from jax.experimental import pallas as pl
from jax.experimental.pallas import tpu as pltpu
from jax.sharding import PartitionSpec as P


def swap_with(value, axis, flip):
    size = lax.axis_size(axis)
    return lax.ppermute(value, axis, [(i, i ^ flip) for i in range(size)])


def from_ahead(value, axis, distance):
    size = lax.axis_size(axis)
    return lax.ppermute(value, axis, [((i + distance) % size, i) for i in range(size)])


def split_code(code, count):
    if count & (count - 1) == 0:
        return code >> (count.bit_length() - 1), code & (count - 1)
    return lax.div(code, count), lax.rem(code, count)


def arrange_kernel(orders, geometry, ids_hbm, counts_hbm, blocks_hbm, *rest):
    side, row_blocks, col_blocks, cols = geometry
    outs, (ids, counts, stage, sems, table_sems) = rest[: len(orders)], rest[len(orders) :]
    slots = stage.shape[1]
    me = lax.axis_index("row")
    shift = (cols - lax.axis_index("col")) * (col_blocks // cols)
    flat = [delta for order in orders for delta in order]
    tables = [
        pltpu.make_async_copy(ids_hbm, ids, table_sems.at[0]),
        pltpu.make_async_copy(counts_hbm, counts, table_sems.at[1]),
    ]
    for table in tables:
        table.start()

    def fetch(spot, delta):
        return pltpu.make_async_copy(blocks_hbm.at[me ^ delta], stage.at[spot], sems.at[spot])

    for spot, delta in enumerate(flat):
        fetch(spot, delta).start()
    if slots != row_blocks * col_blocks:
        for out in outs:
            out[...] = jnp.zeros(out.shape, out.dtype)
    for table in tables:
        table.wait()
    spot = 0
    for out, order in zip(outs, orders):
        for position, delta in enumerate(order):
            segment = me ^ delta
            live = counts[0, segment]
            fetch(spot, delta).wait()
            for slot in range(slots):
                down, across = split_code(ids[slot, segment], col_blocks)
                _, across = split_code(across + shift, col_blocks)
                values = stage[spot, slot]
                values = jnp.where(slot < live, values, jnp.zeros_like(values))
                rows = pl.ds(pl.multiple_of((position * row_blocks + down) * side, side), side)
                lanes = pl.ds(pl.multiple_of(across * side, side), side)
                out[rows, lanes] = values
            spot += 1


def arrange(blocks, block_ids, counts, orders, seg_rows, group_rows):
    segments, slots, side, _ = blocks.shape
    geometry = (side, seg_rows // side, group_rows // side, group_rows // seg_rows)
    total = sum(len(order) for order in orders)
    nbytes = total * seg_rows * group_rows * blocks.dtype.itemsize
    held = nbytes + total * slots * side * side * blocks.dtype.itemsize
    return pl.pallas_call(
        functools.partial(arrange_kernel, orders, geometry),
        out_shape=[jax.ShapeDtypeStruct((len(order) * seg_rows, group_rows), blocks.dtype) for order in orders],
        in_specs=[pl.BlockSpec(memory_space=pltpu.HBM)] * 3,
        out_specs=[pl.BlockSpec(memory_space=pltpu.VMEM) for _ in orders],
        scratch_shapes=[
            pltpu.SMEM((slots, segments), block_ids.dtype),
            pltpu.SMEM((1, segments), counts.dtype),
            pltpu.VMEM((total, slots, side, side), blocks.dtype),
            pltpu.SemaphoreType.DMA((total,)),
            pltpu.SemaphoreType.DMA((2,)),
        ],
        compiler_params=pltpu.CompilerParams(vmem_limit_bytes=held + (4 << 20)),
        cost_estimate=pl.CostEstimate(flops=0, bytes_accessed=2 * nbytes, transcendentals=0),
    )(*[pltpu.with_memory_space_constraint(v, pltpu.HBM) for v in (block_ids.T, counts.T, blocks)])


def local(features, degrees, blocks, block_ids, counts, weight, out_bias):
    seg_rows, width = features.shape
    rows, cols = lax.axis_size("row"), lax.axis_size("col")
    high = rows // 8

    moved = [
        (from_ahead(features, "col", step), from_ahead(degrees, "col", step)) for step in range(1, cols)
    ]

    def scale(rows_in, counts_in):
        scaling = lax.rsqrt(counts_in.astype(jnp.float32))[:, None]
        return (rows_in.astype(jnp.float32) * scaling).astype(jnp.bfloat16), scaling

    scaled, scaling = scale(features, degrees)
    parts = [scaled] + [lax.optimization_barrier(scale(*pair)[0]) for pair in moved]

    far = tuple((h * 4 + q) * 2 for h in range(1, high) for q in range(4))
    near = tuple(q * 2 for q in range(4))
    orders = (tuple(d | 1 for d in far), tuple(d | 1 for d in near), far, near)
    dense = arrange(blocks, block_ids, counts, orders, seg_rows, cols * seg_rows)

    gathered = jnp.concatenate(parts, axis=0)

    def term(matrix):
        product = jnp.dot(matrix, gathered, preferred_element_type=jnp.float32).astype(jnp.bfloat16)
        return product.reshape(-1, seg_rows, width)

    def add(*values):
        return functools.reduce(jnp.add, [v.astype(jnp.float32) for v in values])

    sent_far = swap_with(term(dense[0]), "row", 1)
    sent_near = swap_with(term(dense[1]), "row", 1)
    chip_far = add(term(dense[2]), sent_far).astype(jnp.bfloat16).reshape(high - 1, 4, seg_rows, width)
    chip_near = add(term(dense[3]), sent_near)
    got_far = [swap_with(chip_far[:, q], "row", 2 * q) for q in range(1, 4)]
    got_near = [swap_with(chip_near[q].astype(jnp.bfloat16), "row", 2 * q) for q in range(1, 4)]
    quad_far = add(chip_far[:, 0], *got_far).astype(jnp.bfloat16)
    own = add(chip_near[0], *got_near)
    for h in range(1, high):
        own = own + swap_with(quad_far[h - 1], "row", 8 * h).astype(jnp.float32)

    combined = (scaling * (own + scaled.astype(jnp.float32))).astype(jnp.bfloat16)
    mixed = jnp.dot(combined, weight, preferred_element_type=jnp.float32) + out_bias
    return jnp.maximum(mixed, 0.0).astype(jnp.bfloat16)


def solution(mesh):
    placed = (
        P(("row", "col"), None),
        P(("row", "col")),
        P("row", "col", None, None),
        P("row", "col"),
        P("row", "col"),
        P(),
        P(),
    )
    return jax.shard_map(
        local, mesh=mesh, in_specs=placed, out_specs=P(("row", "col"), None), check_vma=False
    )
```

```python
import functools

import jax
import jax.numpy as jnp
from jax import lax
from jax.experimental import pallas as pl
from jax.experimental.pallas import tpu as pltpu
from jax.sharding import PartitionSpec as P


def swap_with(value, axis, flip):
    size = lax.axis_size(axis)
    return lax.ppermute(value, axis, [(i, i ^ flip) for i in range(size)])


def from_ahead(value, axis, distance):
    size = lax.axis_size(axis)
    return lax.ppermute(value, axis, [((i + distance) % size, i) for i in range(size)])


def split_code(code, count):
    if count & (count - 1) == 0:
        return code >> (count.bit_length() - 1), code & (count - 1)
    return lax.div(code, count), lax.rem(code, count)


def arrange_kernel(orders, geometry, ids_hbm, counts_hbm, blocks_hbm, features_hbm, degrees_hbm, *rest):
    side, row_blocks, col_blocks, cols = geometry
    outs, rest = rest[: len(orders)], rest[len(orders) :]
    features_out, degrees_out, ids, counts, stage, sems, table_sems = rest
    slots = stage.shape[1]
    me = lax.axis_index("row")
    shift = (cols - lax.axis_index("col")) * (col_blocks // cols)

    flat = [me ^ delta for order in orders for delta in order]
    tables = [
        pltpu.make_async_copy(ids_hbm, ids, table_sems.at[0]),
        pltpu.make_async_copy(counts_hbm, counts, table_sems.at[1]),
    ]
    passed = [
        pltpu.make_async_copy(features_hbm, features_out, table_sems.at[2]),
        pltpu.make_async_copy(degrees_hbm, degrees_out, table_sems.at[3]),
    ]
    for table in tables:
        table.start()

    def fetch(spot):
        return pltpu.make_async_copy(blocks_hbm.at[flat[spot]], stage.at[spot], sems.at[spot])

    for spot in range(len(flat)):
        fetch(spot).start()
    for copy in passed:
        copy.start()
    if slots != row_blocks * col_blocks:
        for out in outs:
            out[...] = jnp.zeros(out.shape, out.dtype)
    for table in tables:
        table.wait()
    spot = 0
    for out, order in zip(outs, orders):
        for position in range(len(order)):
            segment = flat[spot]
            live = counts[0, segment]
            fetch(spot).wait()
            for slot in range(slots):
                down, across = split_code(ids[slot, segment], col_blocks)
                _, across = split_code(across + shift, col_blocks)
                values = stage[spot, slot]
                values = jnp.where(slot < live, values, jnp.zeros_like(values))
                rows = pl.ds(pl.multiple_of((position * row_blocks + down) * side, side), side)
                lanes = pl.ds(pl.multiple_of(across * side, side), side)
                out[rows, lanes] = values
            spot += 1
    for copy in passed:
        copy.wait()


def arrange(blocks, block_ids, counts, features, degrees, orders, group_rows):
    seg_rows = features.shape[0]
    segments, slots, side, _ = blocks.shape
    geometry = (side, seg_rows // side, group_rows // side, group_rows // seg_rows)
    total = sum(len(order) for order in orders)
    nbytes = total * seg_rows * group_rows * blocks.dtype.itemsize
    held = nbytes + total * slots * side * side * blocks.dtype.itemsize
    return pl.pallas_call(
        functools.partial(arrange_kernel, orders, geometry),
        out_shape=[jax.ShapeDtypeStruct((len(order) * seg_rows, group_rows), blocks.dtype) for order in orders]
        + [jax.ShapeDtypeStruct(v.shape, v.dtype) for v in (features, degrees)],
        in_specs=[pl.BlockSpec(memory_space=pltpu.HBM)] * 5,
        out_specs=[pl.BlockSpec(memory_space=pltpu.VMEM)] * (len(orders) + 2),
        scratch_shapes=[
            pltpu.SMEM((slots, segments), block_ids.dtype),
            pltpu.SMEM((1, segments), counts.dtype),
            pltpu.VMEM((total, slots, side, side), blocks.dtype),
            pltpu.SemaphoreType.DMA((total,)),
            pltpu.SemaphoreType.DMA((4,)),
        ],
        compiler_params=pltpu.CompilerParams(vmem_limit_bytes=held + (4 << 20)),
        cost_estimate=pl.CostEstimate(flops=0, bytes_accessed=2 * nbytes, transcendentals=0),
    )(*[
        pltpu.with_memory_space_constraint(v, pltpu.HBM)
        for v in (block_ids.T, counts.T, blocks, features, degrees)
    ])


def add(*values):
    return functools.reduce(jnp.add, [v.astype(jnp.float32) for v in values])


def narrow(value):
    return value.astype(jnp.bfloat16)


def local(features, degrees, blocks, block_ids, counts, weight, out_bias):
    seg_rows, width = features.shape
    rows, cols = lax.axis_size("row"), lax.axis_size("col")
    high = rows // 8

    moved = []
    for step in range(1, cols):
        features_in = from_ahead(features, "col", step)
        degrees_in = from_ahead(degrees, "col", step)
        moved.append((features_in, degrees_in))

    first = [h * 8 + q * 2 for q in (1, 2, 3) for h in range(1, high)]
    rest = [h * 8 for h in range(1, high)] + [q * 2 for q in range(4)]
    orders = [[delta | other for delta in part] for part in (first, rest) for other in (1, 0)]
    *dense, features, degrees = arrange(
        blocks, block_ids, counts, features, degrees, orders, cols * seg_rows
    )

    def scale(rows_in, counts_in):
        scaling = lax.rsqrt(counts_in.astype(jnp.float32))[:, None]
        return lax.optimization_barrier((rows_in.astype(jnp.float32) * scaling).astype(jnp.bfloat16))

    parts = [scale(features, degrees)] + [scale(*pair) for pair in moved]
    gathered = jnp.concatenate(parts, axis=0)

    def term(matrix):
        product = jnp.dot(matrix, gathered, preferred_element_type=jnp.float32).astype(jnp.bfloat16)
        return product.reshape(-1, seg_rows, width)

    def over_cores(mine, others):
        to_send = term(others)
        sent = swap_with(to_send, "row", 1)
        kept = term(mine)
        return narrow(add(kept, sent))

    chip_first = over_cores(dense[1], dense[0]).reshape(3, high - 1, seg_rows, width)
    got_far = []
    for q in (1, 3, 2):
        got_far.append(swap_with(chip_first[q - 1], "row", 2 * q))

    chip_rest = over_cores(dense[3], dense[2])
    chip_far, chip_near = chip_rest[: high - 1], chip_rest[high - 1 :]
    quad_far = narrow(add(chip_far, *got_far))
    across = []
    for h in range(1, high):
        across.append(swap_with(quad_far[h - 1], "row", 8 * h))

    got_near = []
    for q in (1, 3, 2):
        got_near.append(swap_with(chip_near[q], "row", 2 * q))

    own = add(chip_near[0], *got_near, *across)
    scaling = lax.rsqrt(degrees.astype(jnp.float32))[:, None]
    combined = (scaling * (own + parts[0].astype(jnp.float32))).astype(jnp.bfloat16)
    mixed = jnp.dot(combined, weight, preferred_element_type=jnp.float32) + out_bias
    return jnp.maximum(mixed, 0.0).astype(jnp.bfloat16)


def solution(mesh):
    placed = (
        P(("row", "col"), None),
        P(("row", "col")),
        P("row", "col", None, None),
        P("row", "col"),
        P("row", "col"),
        P(),
        P(),
    )

    return jax.shard_map(local, mesh=mesh, in_specs=placed, out_specs=P(("row", "col"), None), check_vma=False)
```

```python
import functools

import jax
import jax.numpy as jnp
from jax import lax
from jax.experimental import pallas as pl
from jax.experimental.pallas import tpu as pltpu
from jax.sharding import PartitionSpec as P


def swap_with(value, axis, flip):
    size = lax.axis_size(axis)
    return lax.ppermute(value, axis, [(i, i ^ flip) for i in range(size)])


def from_ahead(value, axis, distance):
    size = lax.axis_size(axis)
    return lax.ppermute(value, axis, [((i + distance) % size, i) for i in range(size)])


def split_code(code, count):
    if count & (count - 1) == 0:
        return code >> (count.bit_length() - 1), code & (count - 1)
    return lax.div(code, count), lax.rem(code, count)


def arrange_kernel(orders, geometry, ids_hbm, counts_hbm, blocks_hbm, features_hbm, degrees_hbm, *rest):
    side, row_blocks, col_blocks, cols = geometry
    outs, rest = rest[: len(orders)], rest[len(orders) :]
    features_out, degrees_out, ids, counts, stage, sems, table_sems = rest
    slots = stage.shape[1]
    me = lax.axis_index("row")
    shift = (cols - lax.axis_index("col")) * (col_blocks // cols)

    flat = [me ^ delta for order in orders for delta in order]
    tables = [
        pltpu.make_async_copy(ids_hbm, ids, table_sems.at[0]),
        pltpu.make_async_copy(counts_hbm, counts, table_sems.at[1]),
    ]
    passed = [
        pltpu.make_async_copy(features_hbm, features_out, table_sems.at[2]),
        pltpu.make_async_copy(degrees_hbm, degrees_out, table_sems.at[3]),
    ]
    for table in tables:
        table.start()

    def fetch(spot):
        return pltpu.make_async_copy(blocks_hbm.at[flat[spot]], stage.at[spot], sems.at[spot])

    for spot in range(len(flat)):
        fetch(spot).start()
    for copy in passed:
        copy.start()
    if slots != row_blocks * col_blocks:
        for out in outs:
            out[...] = jnp.zeros(out.shape, out.dtype)
    for table in tables:
        table.wait()
    spot = 0
    for out, order in zip(outs, orders):
        for position in range(len(order)):
            segment = flat[spot]
            live = counts[0, segment]
            fetch(spot).wait()
            for slot in range(slots):
                down, across = split_code(ids[slot, segment], col_blocks)
                _, across = split_code(across + shift, col_blocks)
                values = stage[spot, slot]
                values = jnp.where(slot < live, values, jnp.zeros_like(values))
                rows = pl.ds(pl.multiple_of((position * row_blocks + down) * side, side), side)
                lanes = pl.ds(pl.multiple_of(across * side, side), side)
                out[rows, lanes] = values
            spot += 1
    for copy in passed:
        copy.wait()


def arrange(blocks, block_ids, counts, features, degrees, orders, group_rows):
    seg_rows = features.shape[0]
    segments, slots, side, _ = blocks.shape
    geometry = (side, seg_rows // side, group_rows // side, group_rows // seg_rows)
    total = sum(len(order) for order in orders)
    nbytes = total * seg_rows * group_rows * blocks.dtype.itemsize
    held = nbytes + total * slots * side * side * blocks.dtype.itemsize
    return pl.pallas_call(
        functools.partial(arrange_kernel, orders, geometry),
        out_shape=[jax.ShapeDtypeStruct((len(order) * seg_rows, group_rows), blocks.dtype) for order in orders]
        + [jax.ShapeDtypeStruct(v.shape, v.dtype) for v in (features, degrees)],
        in_specs=[pl.BlockSpec(memory_space=pltpu.HBM)] * 5,
        out_specs=[pl.BlockSpec(memory_space=pltpu.VMEM)] * (len(orders) + 2),
        scratch_shapes=[
            pltpu.SMEM((slots, segments), block_ids.dtype),
            pltpu.SMEM((1, segments), counts.dtype),
            pltpu.VMEM((total, slots, side, side), blocks.dtype),
            pltpu.SemaphoreType.DMA((total,)),
            pltpu.SemaphoreType.DMA((4,)),
        ],
        compiler_params=pltpu.CompilerParams(vmem_limit_bytes=held + (4 << 20)),
        cost_estimate=pl.CostEstimate(flops=0, bytes_accessed=2 * nbytes, transcendentals=0),
    )(*[
        pltpu.with_memory_space_constraint(v, pltpu.HBM)
        for v in (block_ids.T, counts.T, blocks, features, degrees)
    ])


def add(*values):
    return functools.reduce(jnp.add, [v.astype(jnp.float32) for v in values])


def narrow(value):
    return value.astype(jnp.bfloat16)


def local(features, degrees, blocks, block_ids, counts, weight, out_bias):
    seg_rows, width = features.shape
    rows, cols = lax.axis_size("row"), lax.axis_size("col")
    high = rows // 8

    moved = []
    for step in range(1, cols):
        features_in = from_ahead(features, "col", step)
        degrees_in = from_ahead(degrees, "col", step)
        moved.append((features_in, degrees_in))

    first = [h * 8 + q * 2 for q in (1, 2, 3) for h in range(1, high)]
    rest = [h * 8 for h in range(1, high)] + [q * 2 for q in range(4)]
    orders = [[delta | other for delta in part] for part in (first, rest) for other in (1, 0)]
    *dense, features, degrees = arrange(
        blocks, block_ids, counts, features, degrees, orders, cols * seg_rows
    )

    def scale(rows_in, counts_in):
        scaling = lax.rsqrt(counts_in.astype(jnp.float32))[:, None]
        return lax.optimization_barrier((rows_in.astype(jnp.float32) * scaling).astype(jnp.bfloat16))

    parts = [scale(features, degrees)] + [scale(*pair) for pair in moved]
    gathered = jnp.concatenate(parts[1:], axis=0)

    def product(matrix, features_in):
        return jnp.dot(matrix, features_in, preferred_element_type=jnp.float32)

    def term(at):
        if at < 2:
            ahead = lax.optimization_barrier(product(dense[at][:, :seg_rows], parts[0]))
            total = ahead + product(dense[at][:, seg_rows:], gathered)
        else:
            total = product(dense[at], jnp.concatenate(parts, axis=0))
        return narrow(total).reshape(-1, seg_rows, width)

    def over_cores(mine, others):
        to_send = term(others)
        sent = swap_with(to_send, "row", 1)
        kept = term(mine)
        return narrow(add(kept, sent))

    chip_first = over_cores(1, 0).reshape(3, high - 1, seg_rows, width)
    got_far = []
    for q in (1, 3, 2):
        got_far.append(swap_with(chip_first[q - 1], "row", 2 * q))

    chip_rest = over_cores(3, 2)
    chip_far, chip_near = chip_rest[: high - 1], chip_rest[high - 1 :]
    quad_far = narrow(add(chip_far, *got_far))
    across = []
    for h in range(1, high):
        across.append(swap_with(quad_far[h - 1], "row", 8 * h))

    got_near = []
    for q in (1, 3, 2):
        got_near.append(swap_with(chip_near[q], "row", 2 * q))

    own = add(chip_near[0], *got_near, *across)
    scaling = lax.rsqrt(degrees.astype(jnp.float32))[:, None]
    combined = (scaling * (own + parts[0].astype(jnp.float32))).astype(jnp.bfloat16)
    mixed = jnp.dot(combined, weight, preferred_element_type=jnp.float32) + out_bias
    return jnp.maximum(mixed, 0.0).astype(jnp.bfloat16)


def solution(mesh):
    placed = (
        P(("row", "col"), None),
        P(("row", "col")),
        P("row", "col", None, None),
        P("row", "col"),
        P("row", "col"),
        P(),
        P(),
    )

    return jax.shard_map(local, mesh=mesh, in_specs=placed, out_specs=P(("row", "col"), None), check_vma=False)
```

```python
import functools

import jax
import jax.numpy as jnp
from jax import lax
from jax.experimental import pallas as pl
from jax.experimental.pallas import tpu as pltpu
from jax.sharding import PartitionSpec as P


def swap_with(value, axis, flip):
    size = lax.axis_size(axis)
    return lax.ppermute(value, axis, [(i, i ^ flip) for i in range(size)])


def from_ahead(value, axis, distance):
    size = lax.axis_size(axis)
    return lax.ppermute(value, axis, [((i + distance) % size, i) for i in range(size)])


def split_code(code, count):
    if count & (count - 1) == 0:
        return code >> (count.bit_length() - 1), code & (count - 1)
    return lax.div(code, count), lax.rem(code, count)


def arrange_kernel(orders, geometry, ids_hbm, counts_hbm, blocks_hbm, features_hbm, degrees_hbm, *rest):
    side, row_blocks, col_blocks, cols = geometry
    outs, rest = rest[: len(orders)], rest[len(orders) :]
    features_out, degrees_out, ids, counts, stage, sems, table_sems = rest
    slots = stage.shape[1]
    me = lax.axis_index("row")
    shift = (cols - lax.axis_index("col")) * (col_blocks // cols)

    flat = [me ^ delta for order in orders for delta in order]
    tables = [
        pltpu.make_async_copy(ids_hbm, ids, table_sems.at[0]),
        pltpu.make_async_copy(counts_hbm, counts, table_sems.at[1]),
    ]
    passed = [
        pltpu.make_async_copy(features_hbm, features_out, table_sems.at[2]),
        pltpu.make_async_copy(degrees_hbm, degrees_out, table_sems.at[3]),
    ]
    for table in tables:
        table.start()

    def fetch(spot):
        return pltpu.make_async_copy(blocks_hbm.at[flat[spot]], stage.at[spot], sems.at[spot])

    for spot in range(len(flat)):
        fetch(spot).start()
    for copy in passed:
        copy.start()
    if slots != row_blocks * col_blocks:
        for out in outs:
            out[...] = jnp.zeros(out.shape, out.dtype)
    for table in tables:
        table.wait()
    spot = 0
    for out, order in zip(outs, orders):
        for position in range(len(order)):
            segment = flat[spot]
            live = counts[0, segment]
            fetch(spot).wait()
            for slot in range(slots):
                down, across = split_code(ids[slot, segment], col_blocks)
                _, across = split_code(across + shift, col_blocks)
                values = stage[spot, slot]
                values = jnp.where(slot < live, values, jnp.zeros_like(values))
                rows = pl.ds(pl.multiple_of((position * row_blocks + down) * side, side), side)
                lanes = pl.ds(pl.multiple_of(across * side, side), side)
                out[rows, lanes] = values
            spot += 1
    for copy in passed:
        copy.wait()


def arrange(blocks, block_ids, counts, features, degrees, orders, group_rows):
    seg_rows = features.shape[0]
    segments, slots, side, _ = blocks.shape
    geometry = (side, seg_rows // side, group_rows // side, group_rows // seg_rows)
    total = sum(len(order) for order in orders)
    nbytes = total * seg_rows * group_rows * blocks.dtype.itemsize
    held = nbytes + total * slots * side * side * blocks.dtype.itemsize
    return pl.pallas_call(
        functools.partial(arrange_kernel, orders, geometry),
        out_shape=[jax.ShapeDtypeStruct((len(order) * seg_rows, group_rows), blocks.dtype) for order in orders]
        + [jax.ShapeDtypeStruct(v.shape, v.dtype) for v in (features, degrees)],
        in_specs=[pl.BlockSpec(memory_space=pltpu.HBM)] * 5,
        out_specs=[pl.BlockSpec(memory_space=pltpu.VMEM)] * (len(orders) + 2),
        scratch_shapes=[
            pltpu.SMEM((slots, segments), block_ids.dtype),
            pltpu.SMEM((1, segments), counts.dtype),
            pltpu.VMEM((total, slots, side, side), blocks.dtype),
            pltpu.SemaphoreType.DMA((total,)),
            pltpu.SemaphoreType.DMA((4,)),
        ],
        compiler_params=pltpu.CompilerParams(vmem_limit_bytes=held + (4 << 20)),
        cost_estimate=pl.CostEstimate(flops=0, bytes_accessed=2 * nbytes, transcendentals=0),
    )(*[
        pltpu.with_memory_space_constraint(v, pltpu.HBM)
        for v in (block_ids.T, counts.T, blocks, features, degrees)
    ])


def add(*values):
    return functools.reduce(jnp.add, [v.astype(jnp.float32) for v in values])


def narrow(value):
    return value.astype(jnp.bfloat16)


def local(features, degrees, blocks, block_ids, counts, weight, out_bias):
    seg_rows, width = features.shape
    rows, cols = lax.axis_size("row"), lax.axis_size("col")
    high = rows // 8

    moved = []
    for step in range(1, cols):
        features_in = from_ahead(features, "col", step)
        degrees_in = from_ahead(degrees, "col", step)
        moved.append((features_in, degrees_in))

    far = {q: [h * 8 + q * 2 for h in range(1, high)] for q in range(4)}
    first, second, rest = far[3], far[2] + far[1], far[0] + [q * 2 for q in range(4)]
    orders = [[delta | other for delta in part] for part in (first, second, rest) for other in (1, 0)]
    *dense, features, degrees = arrange(
        blocks, block_ids, counts, features, degrees, orders, cols * seg_rows
    )

    def scale(rows_in, counts_in):
        scaling = lax.rsqrt(counts_in.astype(jnp.float32))[:, None]
        return lax.optimization_barrier((rows_in.astype(jnp.float32) * scaling).astype(jnp.bfloat16))

    parts = [scale(features, degrees)] + [scale(*pair) for pair in moved]
    gathered = jnp.concatenate(parts[1:], axis=0)

    def product(matrix, features_in):
        return jnp.dot(matrix, features_in, preferred_element_type=jnp.float32)

    ahead = [lax.optimization_barrier(product(matrix[:, :seg_rows], parts[0])) for matrix in dense[:4]]

    def term(at):
        if at < len(ahead):
            total = ahead[at] + product(dense[at][:, seg_rows:], gathered)
        else:
            total = product(dense[at], jnp.concatenate(parts, axis=0))
        return narrow(total).reshape(-1, seg_rows, width)

    def over_cores(mine, others):
        to_send = term(others)
        sent = swap_with(to_send, "row", 1)
        kept = term(mine)
        return narrow(add(kept, sent))

    leaving = {3: over_cores(1, 0)}
    both = over_cores(3, 2)
    leaving[2], leaving[1] = both[: high - 1], both[high - 1 :]
    got_far = []
    for q in (3, 2, 1):
        got_far.append(swap_with(leaving[q], "row", 2 * q))

    chip_rest = over_cores(5, 4)
    chip_far, chip_near = chip_rest[: high - 1], chip_rest[high - 1 :]
    quad_far = narrow(add(chip_far, *got_far))
    across = []
    for h in range(1, high):
        across.append(swap_with(quad_far[h - 1], "row", 8 * h))

    got_near = []
    for q in (1, 3, 2):
        got_near.append(swap_with(chip_near[q], "row", 2 * q))

    own = add(chip_near[0], *got_near, *across)
    scaling = lax.rsqrt(degrees.astype(jnp.float32))[:, None]
    combined = (scaling * (own + parts[0].astype(jnp.float32))).astype(jnp.bfloat16)
    mixed = jnp.dot(combined, weight, preferred_element_type=jnp.float32) + out_bias
    return jnp.maximum(mixed, 0.0).astype(jnp.bfloat16)


def solution(mesh):
    placed = (
        P(("row", "col"), None),
        P(("row", "col")),
        P("row", "col", None, None),
        P("row", "col"),
        P("row", "col"),
        P(),
        P(),
    )

    return jax.shard_map(local, mesh=mesh, in_specs=placed, out_specs=P(("row", "col"), None), check_vma=False)
```

```python
import functools

import jax
import jax.numpy as jnp
from jax import lax
from jax.experimental import pallas as pl
from jax.experimental.pallas import tpu as pltpu
from jax.sharding import PartitionSpec as P


def swap_with(value, axis, flip):
    size = lax.axis_size(axis)
    return lax.ppermute(value, axis, [(i, i ^ flip) for i in range(size)])


def from_ahead(value, axis, distance):
    size = lax.axis_size(axis)
    return lax.ppermute(value, axis, [((i + distance) % size, i) for i in range(size)])


def split_code(code, count):
    if count & (count - 1) == 0:
        return code >> (count.bit_length() - 1), code & (count - 1)
    return lax.div(code, count), lax.rem(code, count)


def arrange_kernel(orders, geometry, ids_hbm, counts_hbm, blocks_hbm, features_hbm, degrees_hbm, *rest):
    side, row_blocks, col_blocks, cols = geometry
    outs, rest = rest[: len(orders)], rest[len(orders) :]
    features_out, degrees_out, ids, counts, stage, sems, table_sems = rest
    slots = stage.shape[1]
    me = lax.axis_index("row")
    shift = (cols - lax.axis_index("col")) * (col_blocks // cols)

    flat = [me ^ delta for order in orders for delta in order]
    tables = [
        pltpu.make_async_copy(ids_hbm, ids, table_sems.at[0]),
        pltpu.make_async_copy(counts_hbm, counts, table_sems.at[1]),
    ]
    passed = [
        pltpu.make_async_copy(features_hbm, features_out, table_sems.at[2]),
        pltpu.make_async_copy(degrees_hbm, degrees_out, table_sems.at[3]),
    ]
    for table in tables:
        table.start()

    def fetch(spot):
        return pltpu.make_async_copy(blocks_hbm.at[flat[spot]], stage.at[spot], sems.at[spot])

    for spot in range(len(flat)):
        fetch(spot).start()
    for copy in passed:
        copy.start()
    if slots != row_blocks * col_blocks:
        for out in outs:
            out[...] = jnp.zeros(out.shape, out.dtype)
    for table in tables:
        table.wait()
    spot = 0
    for out, order in zip(outs, orders):
        for position in range(len(order)):
            segment = flat[spot]
            live = counts[0, segment]
            fetch(spot).wait()
            for slot in range(slots):
                down, across = split_code(ids[slot, segment], col_blocks)
                _, across = split_code(across + shift, col_blocks)
                values = stage[spot, slot]
                values = jnp.where(slot < live, values, jnp.zeros_like(values))
                rows = pl.ds(pl.multiple_of((position * row_blocks + down) * side, side), side)
                lanes = pl.ds(pl.multiple_of(across * side, side), side)
                out[rows, lanes] = values
            spot += 1
    for copy in passed:
        copy.wait()


def arrange(blocks, block_ids, counts, features, degrees, orders, group_rows):
    seg_rows = features.shape[0]
    segments, slots, side, _ = blocks.shape
    geometry = (side, seg_rows // side, group_rows // side, group_rows // seg_rows)
    total = sum(len(order) for order in orders)
    nbytes = total * seg_rows * group_rows * blocks.dtype.itemsize
    held = nbytes + total * slots * side * side * blocks.dtype.itemsize
    return pl.pallas_call(
        functools.partial(arrange_kernel, orders, geometry),
        out_shape=[jax.ShapeDtypeStruct((len(order) * seg_rows, group_rows), blocks.dtype) for order in orders]
        + [jax.ShapeDtypeStruct(v.shape, v.dtype) for v in (features, degrees)],
        in_specs=[pl.BlockSpec(memory_space=pltpu.HBM)] * 5,
        out_specs=[pl.BlockSpec(memory_space=pltpu.VMEM)] * (len(orders) + 2),
        scratch_shapes=[
            pltpu.SMEM((slots, segments), block_ids.dtype),
            pltpu.SMEM((1, segments), counts.dtype),
            pltpu.VMEM((total, slots, side, side), blocks.dtype),
            pltpu.SemaphoreType.DMA((total,)),
            pltpu.SemaphoreType.DMA((4,)),
        ],
        compiler_params=pltpu.CompilerParams(vmem_limit_bytes=held + (4 << 20)),
        cost_estimate=pl.CostEstimate(flops=0, bytes_accessed=2 * nbytes, transcendentals=0),
    )(*[
        pltpu.with_memory_space_constraint(v, pltpu.HBM)
        for v in (block_ids.T, counts.T, blocks, features, degrees)
    ])


def add(*values):
    return functools.reduce(jnp.add, [v.astype(jnp.float32) for v in values])


def narrow(value):
    return value.astype(jnp.bfloat16)


def local(features, degrees, blocks, block_ids, counts, weight, out_bias):
    seg_rows, width = features.shape
    rows, cols = lax.axis_size("row"), lax.axis_size("col")
    high = rows // 8

    moved = []
    for step in range(1, cols):
        features_in = from_ahead(features, "col", step)
        degrees_in = from_ahead(degrees, "col", step)
        moved.append((features_in, degrees_in))

    far = {q: [h * 8 + q * 2 for h in range(1, high)] for q in range(4)}
    first, second = far[3], far[2] + far[1] + far[0] + [q * 2 for q in range(4)]
    orders = [[delta | other for delta in part] for part in (first, second) for other in (1, 0)]
    *dense, features, degrees = arrange(
        blocks, block_ids, counts, features, degrees, orders, cols * seg_rows
    )

    def scale(rows_in, counts_in):
        scaling = lax.rsqrt(counts_in.astype(jnp.float32))[:, None]
        return lax.optimization_barrier((rows_in.astype(jnp.float32) * scaling).astype(jnp.bfloat16))

    parts = [scale(features, degrees)] + [scale(*pair) for pair in moved]
    gathered = jnp.concatenate(parts[1:], axis=0)

    def product(matrix, features_in):
        return jnp.dot(matrix, features_in, preferred_element_type=jnp.float32)

    ahead = [lax.optimization_barrier(product(matrix[:, :seg_rows], parts[0])) for matrix in dense[:2]]

    def term(at):
        if at < len(ahead):
            total = ahead[at] + product(dense[at][:, seg_rows:], gathered)
        else:
            total = product(dense[at], jnp.concatenate(parts, axis=0))
        return narrow(total).reshape(-1, seg_rows, width)

    def over_cores(mine, others):
        to_send = term(others)
        sent = swap_with(to_send, "row", 1)
        kept = term(mine)
        return narrow(add(kept, sent))

    leaving = {3: over_cores(1, 0)}
    both = over_cores(3, 2)
    count = high - 1
    leaving[2], leaving[1] = both[:count], both[count : 2 * count]
    chip_far, chip_near = both[2 * count : 3 * count], both[3 * count :]
    got_far = []
    for q in (3, 2, 1):
        got_far.append(swap_with(leaving[q], "row", 2 * q))

    quad_far = narrow(add(chip_far, *got_far))
    across = []
    for h in range(1, high):
        across.append(swap_with(quad_far[h - 1], "row", 8 * h))

    got_near = []
    for q in (1, 3, 2):
        got_near.append(swap_with(chip_near[q], "row", 2 * q))

    own = add(chip_near[0], *got_near, *across)
    scaling = lax.rsqrt(degrees.astype(jnp.float32))[:, None]
    combined = (scaling * (own + parts[0].astype(jnp.float32))).astype(jnp.bfloat16)
    mixed = jnp.dot(combined, weight, preferred_element_type=jnp.float32) + out_bias
    return jnp.maximum(mixed, 0.0).astype(jnp.bfloat16)


def solution(mesh):
    placed = (
        P(("row", "col"), None),
        P(("row", "col")),
        P("row", "col", None, None),
        P("row", "col"),
        P("row", "col"),
        P(),
        P(),
    )

    return jax.shard_map(local, mesh=mesh, in_specs=placed, out_specs=P(("row", "col"), None), check_vma=False)
```
